32 devices in a mesh: rows: 8 (over z, y), modes: 4 (over x, core).
Axes of the slice: x: 2, y: 2, z: 4, core: 2. Of those that a mesh axis runs over, the one named last changes fastest.
Arguments:
- basis: float32 [16384, 16384], P('rows', 'modes'), may hold values from -0.046875 to 0.046875
- blocks: float32 [3, 16384, 256], P(None, ('rows', 'modes')), may hold values from -6 to 6
Outputs:
- projected: float32 [3, 16384, 256], P(None, ('rows', 'modes'))
The draws below stay inside these ranges and needn't reach their ends.
All inputs are finite; a program needn't handle non-finite values.
Results may differ from the reference program's by a relative error of at most 0.0001.
Values sent between devices are 32-bit elements; how exact they have to be, the bound alone decides.
A program may use at most 192 MiB of HBM per device.

```python
import jax
import jax.numpy as jnp
from jax import lax

M = 16384
K = 256
BLOCKS = 3
NROWS = 16384


def shard_levels(own_key, shape, shards, low, high):
    loudness, own = 1.0, jax.random.fold_in(own_key, 6)
    for axis_at, shards_of in shards:
        heights = jnp.exp(jax.random.uniform(jax.random.fold_in(own, axis_at), (shards_of,), jnp.float32, low / len(shards), high / len(shards)))
        loudness = loudness * jnp.repeat(heights, shape[axis_at] // shards_of).reshape([-1 if axis == axis_at else 1 for axis in range(len(shape))])
    return loudness


def gaussian(own_key, extent, deviation, most, shards=(), held_as=jnp.bfloat16):
    result = deviation * jax.random.normal(own_key, extent, jnp.float32)
    if shards:
        result = result * shard_levels(own_key, extent, shards, -0.22, 0.18)
    return jnp.clip(result, -most, most).astype(held_as)


def setup_inputs(seed: int = 0) -> dict:
    key_list = jax.random.split(jax.random.key(seed), 3)
    return {
        "basis": gaussian(key_list[0], (NROWS, M), NROWS ** -0.5, 0.046875, ((0, 8), (1, 4)), jnp.float32),
        "blocks": gaussian(key_list[1], (BLOCKS, NROWS, K), 1.0, 6.0, ((1, 32),), jnp.float32),
    }


def project_block(basis, block_rows):
    coefficients = lax.dot_general(basis, block_rows, (((0,), (0,)), ((), ())), precision=lax.Precision.HIGHEST, preferred_element_type=jnp.float32)
    correction = jnp.dot(basis, coefficients, precision=lax.Precision.HIGHEST, preferred_element_type=jnp.float32)
    return block_rows - correction


def reference(basis, blocks):
    results = []
    for block_index in range(BLOCKS):
        results.append(project_block(basis, blocks[block_index]))
    return jnp.stack(results)
```

```python
import jax
import jax.numpy as jnp
from jax import lax
from jax.sharding import PartitionSpec as P


def bit_of(axis, bit):
    return (lax.axis_index(axis) // (1 << bit)) % 2


def swap(value, axis, size, bit):
    return lax.ppermute(value, axis, [(i, i ^ (1 << bit)) for i in range(size)])


def levels(size):
    assert size & (size - 1) == 0
    return size.bit_length() - 1


def gather(value, axis, size):
    count = levels(size)
    rows, columns = value.shape
    for at, bit in enumerate(reversed(range(count))):
        mine = bit_of(axis, bit)
        other = swap(value, axis, size, bit)
        value = jnp.stack(
            [jnp.where(mine == 0, value, other), jnp.where(mine == 0, other, value)], axis=at
        )
    return value.reshape(size * rows, columns)


def scatter_sum(value, axis, size):
    count = levels(size)
    rows, columns = value.shape
    value = value.reshape((2,) * count + (rows // size, columns))
    for bit in range(count):
        mine = bit_of(axis, bit)
        at = count - 1 - bit
        sent = lax.dynamic_index_in_dim(value, 1 - mine, at, keepdims=False)
        kept = lax.dynamic_index_in_dim(value, mine, at, keepdims=False)
        value = kept + swap(sent, axis, size, bit)
    return value


def on_device(modes, basis, blocks):
    high = lax.Precision.HIGH
    count = blocks.shape[0]
    partials, summed = [], []
    for index in range(count):
        partials.append(
            lax.dot_general(
                basis,
                gather(blocks[index], "modes", modes),
                (((0,), (0,)), ((), ())),
                precision=high,
                preferred_element_type=jnp.float32,
            )
        )
    for index in range(count):
        partial_value = partials[index]
        if index:
            summed[-1], partial_value = lax.optimization_barrier((summed[-1], partial_value))
        summed.append(lax.psum(partial_value, "rows"))
    results = []
    for index in range(count):
        correction = jnp.dot(
            basis, summed[index], precision=high, preferred_element_type=jnp.float32
        )
        results.append(blocks[index] - scatter_sum(correction, "modes", modes))
    return jnp.stack(results)


def solution(mesh):
    in_specs = (P("rows", "modes"), P(None, ("rows", "modes"), None))
    out_specs = P(None, ("rows", "modes"), None)
    modes = mesh.shape["modes"]

    def run(basis, blocks):
        return on_device(modes, basis, blocks)

    return jax.shard_map(run, mesh=mesh, in_specs=in_specs, out_specs=out_specs, check_vma=False)
```
